32 devices in a mesh: wide: 16 (over z, y, core), narrow: 2 (over x).
Axes of the slice: x: 2, y: 2, z: 4, core: 2. Of those that a mesh axis runs over, the one named last changes fastest.
Arguments:
- latent: bfloat16 [16, 64, 128], P(None, 'wide'), may hold values from -6 to 6
- land_sea: int32 [64, 128], P('wide'), may hold values 0 or 1
- head_shift: int32 [16, 2], P('narrow'), may hold values from -1 to 1
- logit_scale: float32 [16], P('narrow'), may hold values from 4 to 600
- embed_weight: bfloat16 [16, 1024], replicated, may hold values from -1.5 to 1.5
- land_vector: bfloat16 [1024], replicated, may hold values from -6 to 6
- qkv_weight: bfloat16 [1024, 3, 1024], P(None, None, 'narrow'), may hold values from -0.1875 to 0.1875
- out_weight: bfloat16 [1024, 1024], P('narrow'), may hold values from -0.75 to 0.75
- proj_weight: bfloat16 [1024, 16], replicated, may hold values from -0.1875 to 0.1875
- conv_in_weight: bfloat16 [3, 3, 16, 512], replicated, may hold values from -0.5 to 0.5
- level_one_weight: bfloat16 [3, 3, 512, 512], replicated, may hold values from -0.15625 to 0.15625
- level_two_weight: bfloat16 [3, 3, 512, 256], replicated, may hold values from -0.15625 to 0.15625
- level_three_weight: bfloat16 [3, 3, 256, 128], replicated, may hold values from -0.21875 to 0.21875
- conv_out_weight: bfloat16 [3, 3, 128, 4], replicated, may hold values from -0.3125 to 0.3125
Outputs:
- image: float32 [4, 512, 1024], P(None, 'wide', 'narrow')
The draws below stay inside these ranges and needn't reach their ends.
All inputs are finite; a program needn't handle non-finite values. No bound on the sum of `land_sea` on one device may be relied on, other than what follows from the above.
Results may differ from the reference program's by a relative error of at most 0.025.
Values may be sent and summed in bfloat16 or wider, within the bound.
A program may use at most 256 MiB of HBM per device.

```python
import math
import jax
import jax.numpy as jnp
from jax import lax

C_LAT = 16
D = 1024
HEADS = 16
HD = 64
WIN = 7
CH_A = 512
CH_B = 256
CH_C = 128
OUT_VARS = 4
W = 128
H = 64


def draw_logit_scale(key, part):
    uniform_draw = jax.random.uniform(key, (HEADS,), jnp.float32)
    lowest = 4.0
    highest = 40.0
    return jnp.exp(jnp.log(lowest) + uniform_draw * (jnp.log(highest) - jnp.log(lowest)))


def with_ends(array, stream_key, smallest, high):
    place = [jax.random.randint(jax.random.fold_in(stream_key, axis), (), 0, length) for axis, length in enumerate(array.shape)]
    widest = array.shape.index(max(array.shape))
    neighbour = place[:widest] + [(place[widest] + 1) % array.shape[widest]] + place[widest + 1:]
    return array.at[tuple(place)].set(smallest).at[tuple(neighbour)].set(high)


def levels(key, dims, cuts, low, largest):
    def one(dim, blocks):
        draws = jax.random.uniform(jax.random.fold_in(jax.random.fold_in(key, 6), dim), (blocks,), jnp.float32, low / len(cuts), largest / len(cuts))
        return jnp.repeat(jnp.exp(draws), dims[dim] // blocks).reshape((-1,) + (1,) * (len(dims) - dim - 1))

    loudness = one(*cuts[0])
    for cut in cuts[1:]:
        loudness = loudness * one(*cut)
    return loudness


def bell_draw(rng, shape, width, most, split=(), kind=jnp.bfloat16):
    array = jax.random.normal(rng, shape, jnp.float32) * width
    if len(split) > 0:
        array = levels(rng, shape, split, -0.22, 0.18) * array
    return jnp.clip(array, min=-most, max=most).astype(kind)


def setup_inputs(seed: int = 0) -> dict:
    seeds = jax.random.split(jax.random.key(seed), 15)
    return {
        "latent": bell_draw(seeds[0], (C_LAT, H, W), 1.0, 6.0, ((1, 16),)),
        "land_sea": with_ends((jax.random.randint(seeds[1], (H, W), 0, 10) < 3).astype(jnp.int32), jax.random.fold_in(seeds[1], 1), 0, 1),
        "head_shift": with_ends(jax.random.randint(seeds[2], (HEADS, 2), -1, 2), jax.random.fold_in(seeds[2], 1), -1, 1).astype(jnp.int32),
        "logit_scale": draw_logit_scale(jax.random.fold_in(seeds[14], 71), 0),
        "embed_weight": bell_draw(seeds[4], (C_LAT, D), C_LAT ** -0.5, 1.5),
        "land_vector": bell_draw(seeds[5], (D,), 1.0, 6.0),
        "qkv_weight": bell_draw(seeds[6], (D, 3, D), D ** -0.5, 0.1875, ((2, 2),)),
        "out_weight": bell_draw(seeds[7], (D, D), HD ** -0.5, 0.75, ((0, 2),)),
        "proj_weight": bell_draw(seeds[8], (D, C_LAT), D ** -0.5, 0.1875),
        "conv_in_weight": bell_draw(seeds[9], (3, 3, C_LAT, CH_A), (9 * C_LAT) ** -0.5, 0.5),
        "level_one_weight": bell_draw(seeds[10], (3, 3, CH_A, CH_A), (3 * CH_A) ** -0.5, 0.15625),
        "level_two_weight": bell_draw(seeds[11], (3, 3, CH_A, CH_B), (3 * CH_A) ** -0.5, 0.15625),
        "level_three_weight": bell_draw(seeds[12], (3, 3, CH_B, CH_C), (3 * CH_B) ** -0.5, 0.21875),
        "conv_out_weight": bell_draw(seeds[13], (3, 3, CH_C, OUT_VARS), (3 * CH_C) ** -0.5, 0.3125),
    }


plan_now = 0.3
plan_next = 0.5
keep_factor = math.sqrt(plan_next / plan_now)
noise_factor = math.sqrt(1.0 - plan_next) - keep_factor * math.sqrt(1.0 - plan_now)

def unit_rows(values_in):
    return values_in * lax.rsqrt(lax.optimization_barrier(jnp.sum(values_in * values_in, axis=1, keepdims=True)) + 1e-06)

def window_attend(query_hat, key_pad, value_pad, valid_cells, shifts, scales):
    row_count = query_hat.shape[2]
    col_count = query_hat.shape[3]
    reach = (WIN - 1) // 2
    margin = reach + 1
    offsets = [(row_step, col_step) for row_step in range(-reach, reach + 1) for col_step in range(-reach, reach + 1)]

    def attend_head(query_head, key_head, value_head, shift_pair, scale_head):
        head_dim = query_head.shape[0]
        anchor = jnp.zeros((), jnp.int32)
        shift_row = shift_pair[0].astype(jnp.int32)
        shift_col = shift_pair[1].astype(jnp.int32)
        scores = []
        for row_step, col_step in offsets:
            row_start = (shift_row + (margin + row_step)).astype(jnp.int32)
            col_start = (shift_col + (margin + col_step)).astype(jnp.int32)
            key_block = lax.dynamic_slice(key_head, (anchor, row_start, col_start), (head_dim, row_count, col_count))
            inside = lax.dynamic_slice(valid_cells, (row_start, col_start), (row_count, col_count))
            scores.append(jnp.where(inside, scale_head * lax.optimization_barrier(jnp.sum(query_head * key_block, axis=0)), -jnp.inf))
        scores = jnp.stack(scores)
        row_peak = lax.optimization_barrier(jnp.max(scores, axis=0))
        exponent = jnp.exp(scores - row_peak)
        weights = (exponent / lax.optimization_barrier(jnp.sum(exponent, axis=0))).astype(jnp.bfloat16)
        accumulated = jnp.zeros((head_dim, row_count, col_count), jnp.float32)
        for slot_index, (row_step, col_step) in enumerate(offsets):
            row_start = (shift_row + (margin + row_step)).astype(jnp.int32)
            col_start = (shift_col + (margin + col_step)).astype(jnp.int32)
            value_block = lax.dynamic_slice(value_head, (anchor, row_start, col_start), (head_dim, row_count, col_count))
            accumulated = accumulated + weights[slot_index].astype(jnp.float32) * value_block.astype(jnp.float32)
        return accumulated.astype(jnp.bfloat16)
    return jax.vmap(attend_head)(query_hat, key_pad, value_pad, shifts, scales)

def conv_same(field_in, weight):
    return lax.conv_general_dilated(field_in[None].astype(jnp.float32), weight.astype(jnp.float32), (1, 1), ((1, 1), (1, 1)), dimension_numbers=('NCHW', 'HWIO', 'NCHW'), precision=lax.Precision.HIGHEST)[0]

def widen(field_in):
    channels, row_count, col_count = field_in.shape
    grown = jnp.broadcast_to(field_in[:, :, None, :, None], (channels, row_count, 2, col_count, 2))
    return grown.reshape(channels, 2 * row_count, 2 * col_count)

def reference(latent, land_sea, head_shift, logit_scale, embed_weight, land_vector, qkv_weight, out_weight, proj_weight, conv_in_weight, level_one_weight, level_two_weight, level_three_weight, conv_out_weight):
    highest = lax.Precision.HIGHEST
    land_cells = land_sea.astype(jnp.float32)
    embedded = jnp.einsum('cd,crw->drw', embed_weight.astype(jnp.float32), latent.astype(jnp.float32), precision=highest)
    embedded = (embedded + land_cells[None] * land_vector.astype(jnp.float32)[:, None, None]).astype(jnp.bfloat16)

    def project(part_index):
        flat_proj = jnp.einsum('dm,drw->mrw', qkv_weight[:, part_index].astype(jnp.float32), embedded.astype(jnp.float32), precision=highest)
        return flat_proj.reshape(HEADS, HD, H, W)
    query_hat = unit_rows(project(0))
    key_hat = unit_rows(project(1))
    values = project(2).astype(jnp.bfloat16)
    margin = (WIN - 1) // 2 + 1
    pad_spec = ((0, 0), (0, 0), (margin, margin), (margin, margin))
    key_pad = jnp.pad(key_hat, pad_spec)
    value_pad = jnp.pad(values, pad_spec)
    valid_cells = jnp.pad(jnp.ones((H, W), dtype=bool), margin)
    heads_out = window_attend(query_hat, key_pad, value_pad, valid_cells, head_shift, logit_scale)
    mixed_heads = heads_out.reshape(D, H, W)
    attended = jnp.einsum('md,mrw->drw', out_weight.astype(jnp.float32), mixed_heads.astype(jnp.float32), precision=highest)
    residual_stream = embedded.astype(jnp.float32) + attended
    noise = jnp.einsum('dc,drw->crw', proj_weight.astype(jnp.float32), residual_stream, precision=highest)
    stepped = (keep_factor * latent.astype(jnp.float32) + noise_factor * noise).astype(jnp.bfloat16)
    hidden = jax.nn.silu(conv_same(stepped, conv_in_weight)).astype(jnp.bfloat16)
    for weight in (level_one_weight, level_two_weight, level_three_weight):
        hidden = jax.nn.silu(conv_same(widen(hidden), weight)).astype(jnp.bfloat16)
    return conv_same(hidden, conv_out_weight)
```

```python
import functools
import math

import jax
import jax.numpy as jnp
from jax import lax
from jax.experimental import pallas as pl
from jax.experimental.pallas import tpu as pltpu
from jax.sharding import PartitionSpec as P

WIN = 7
REACH = (WIN - 1) // 2
MARGIN = REACH + 1
HALO = 2


plan_now = 0.3
plan_next = 0.5
keep_factor = math.sqrt(plan_next / plan_now)
noise_factor = math.sqrt(1.0 - plan_next) - keep_factor * math.sqrt(1.0 - plan_now)


def neighbour_rows(cells, width, dim):
    count = lax.axis_size("wide")
    head = lax.slice_in_dim(cells, 0, width, axis=dim)
    tail = lax.slice_in_dim(cells, cells.shape[dim] - width, cells.shape[dim], axis=dim)
    above = lax.ppermute(tail, "wide", [(i, i + 1) for i in range(count - 1)])
    below = lax.ppermute(head, "wide", [(i + 1, i) for i in range(count - 1)])
    return jnp.concatenate([above, cells, below], axis=dim)


def attend_kernel(
    row_count,
    col_count,
    head_dim,
    group,
    shift_ref,
    scale_ref,
    band_ref,
    query_ref,
    key_ref,
    value_ref,
    out_ref,
    query_split,
    key_split,
):
    step = pl.program_id(0)
    span = WIN * col_count
    col_step = lax.broadcasted_iota(jnp.int32, (col_count, col_count), 1) - lax.broadcasted_iota(
        jnp.int32, (col_count, col_count), 0
    )

    def unit(x):
        return x * lax.rsqrt(jnp.sum(x * x, axis=1, keepdims=True) + 1e-06)

    def halves(x):
        high = x.astype(jnp.bfloat16)
        return high, (x - high.astype(jnp.float32)).astype(jnp.bfloat16)

    for slot in range(group):
        head = step * group + slot
        lanes = slice(slot * head_dim, (slot + 1) * head_dim)
        shift_row = shift_ref[head, 0]
        shift_col = shift_ref[head, 1]
        q_high, q_low = halves(unit(query_ref[:, lanes]) * scale_ref[head])
        k_high, k_low = halves(unit(key_ref[:, lanes]))
        query_split[...] = jnp.concatenate([q_high, q_low, q_high, q_low], axis=1)
        key_split[...] = jnp.concatenate([k_high, k_high, k_low, k_low], axis=1)
        offset = col_step - shift_col
        col_bias = jnp.where((offset >= -REACH) & (offset <= REACH), 0.0, -1e30)
        for row in range(row_count):
            start = pl.multiple_of((row + shift_row + (MARGIN - REACH)) * col_count, col_count)
            scores = lax.dot_general(
                query_split[row * col_count : (row + 1) * col_count, :],
                key_split[pl.ds(start, span), :],
                (((1,), (1,)), ((), ())),
                preferred_element_type=jnp.float32,
            )
            first = band_ref[0] + row + shift_row - REACH
            pieces = []
            for k in range(WIN):
                inside = (first + k >= 0) & (first + k < band_ref[1])
                pieces.append(
                    scores[:, k * col_count : (k + 1) * col_count]
                    + (col_bias + jnp.where(inside, 0.0, -1e30))
                )
            peak = jnp.max(functools.reduce(jnp.maximum, pieces), axis=1, keepdims=True)
            pieces = [jnp.exp(piece - peak) for piece in pieces]
            total = jnp.sum(functools.reduce(jnp.add, pieces), axis=1, keepdims=True)
            norm = 1.0 / total
            weights = jnp.concatenate(
                [(piece * norm).astype(jnp.bfloat16) for piece in pieces], axis=1
            )
            mixed = jnp.dot(
                weights, value_ref[pl.ds(start, span), lanes], preferred_element_type=jnp.float32
            )
            out_ref[row * col_count : (row + 1) * col_count, lanes] = mixed.astype(jnp.bfloat16)


def window_attend(query, key, value, shifts, scales, band, row_count, col_count, head_dim):
    heads_here = shifts.shape[0]
    group = 2 if heads_here % 2 == 0 else 1
    width = group * head_dim
    cells = row_count * col_count
    cells_ext = key.shape[0]
    smem = pl.BlockSpec(memory_space=pltpu.SMEM)
    return pl.pallas_call(
        functools.partial(attend_kernel, row_count, col_count, head_dim, group),
        out_shape=jax.ShapeDtypeStruct((cells, heads_here * head_dim), jnp.bfloat16),
        grid=(heads_here // group,),
        in_specs=[
            smem,
            smem,
            smem,
            pl.BlockSpec((cells, width), lambda i: (0, i)),
            pl.BlockSpec((cells_ext, width), lambda i: (0, i)),
            pl.BlockSpec((cells_ext, width), lambda i: (0, i)),
        ],
        out_specs=pl.BlockSpec((cells, width), lambda i: (0, i)),
        scratch_shapes=[
            pltpu.VMEM((cells, 4 * head_dim), jnp.bfloat16),
            pltpu.VMEM((cells_ext, 4 * head_dim), jnp.bfloat16),
        ],
        name="window_attend",
    )(shifts, scales, band, query, key, value)


def corner_weight(weight):
    full = weight.astype(jnp.float32)
    rows = jnp.stack(
        [jnp.stack([full[0] + full[1], full[0]]), jnp.stack([full[2], full[1] + full[2]])]
    )
    left = jnp.stack([rows[:, :, 0] + rows[:, :, 1], rows[:, :, 0]], axis=2)
    right = jnp.stack([rows[:, :, 2], rows[:, :, 1] + rows[:, :, 2]], axis=2)
    taps = jnp.stack([left, right], axis=2)
    taps = jnp.transpose(taps, (0, 2, 4, 1, 3, 5)).astype(jnp.bfloat16)
    return taps.reshape(2, 2, weight.shape[2], 4 * weight.shape[3])


def conv_valid(padded, weight):
    return lax.conv_general_dilated(
        padded[None],
        weight,
        (1, 1),
        "VALID",
        dimension_numbers=("NHWC", "HWIO", "NHWC"),
        preferred_element_type=jnp.float32,
    )[0]


def inside_mask(rows, cols, row_first, col_first, row_total, col_total):
    row_index = row_first + jnp.arange(rows, dtype=jnp.int32)
    col_index = col_first + jnp.arange(cols, dtype=jnp.int32)
    row_in = (row_index >= 0) & (row_index < row_total)
    col_in = (col_index >= 0) & (col_index < col_total)
    return (row_in[:, None] & col_in[None, :])[:, :, None]


def grow(field_in, weight):
    out = jax.nn.silu(conv_valid(field_in, weight)).astype(jnp.bfloat16)
    rows, cols, channels = out.shape
    channels = channels // 4
    out = out.reshape(rows, cols, 2, 2, channels).transpose(0, 2, 1, 3, 4)
    return out.reshape(2 * rows, 2 * cols, channels)


def conv_final(padded, weight):
    rows, cols = padded.shape[0] - 2, padded.shape[1] - 2
    out_vars = weight.shape[3]
    taps = jnp.transpose(weight, (0, 1, 3, 2)).reshape(9 * out_vars, weight.shape[2])
    parts = jnp.einsum("kd,rcd->krc", taps, padded, preferred_element_type=jnp.float32)
    parts = parts.reshape(3, 3, out_vars, rows + 2, cols + 2)
    image = jnp.zeros((out_vars, rows, cols), jnp.float32)
    for a in range(3):
        for b in range(3):
            image = image + parts[a, b, :, a : a + rows, b : b + cols]
    return image


def noise_everywhere(part):
    wide = lax.axis_size("wide")
    narrow = lax.axis_size("narrow")
    rows = part.shape[1]
    pieces = {
        1: lax.slice_in_dim(part, rows - HALO, rows, axis=1),
        0: part,
        -1: lax.slice_in_dim(part, 0, HALO, axis=1),
    }
    sums = {}
    for move in (0, 1, -1):
        total = part if move == 0 else None
        for turn in range(narrow):
            if move == 0 and turn == 0:
                continue
            pairs = [
                (w * narrow + n, (w + move) * narrow + (n + turn) % narrow)
                for w in range(wide)
                for n in range(narrow)
                if 0 <= w + move < wide
            ]
            arrived = lax.ppermute(pieces[move], ("wide", "narrow"), pairs)
            total = arrived if total is None else total + arrived
        sums[move] = total
    return jnp.concatenate([sums[1], sums[0], sums[-1]], axis=1)


def shards(
    latent,
    land_sea,
    head_shift,
    logit_scale,
    embed_weight,
    land_vector,
    qkv_weight,
    out_weight,
    proj_weight,
    conv_in_weight,
    level_one_weight,
    level_two_weight,
    level_three_weight,
    conv_out_weight,
):
    channels, row_count, col_count = latent.shape
    heads_here = head_shift.shape[0]
    head_dim = qkv_weight.shape[2] // heads_here
    cells = row_count * col_count
    band_start = lax.axis_index("wide") * row_count
    total_rows = row_count * lax.axis_size("wide")

    fields = jnp.concatenate([latent, land_sea.astype(jnp.bfloat16)[None]], axis=0)
    fields = neighbour_rows(fields, MARGIN, 1)
    field_weight = jnp.concatenate([embed_weight, land_vector[None]], axis=0)
    rows_ext = row_count + 2 * MARGIN
    embedded = jnp.einsum(
        "cm,cd->md",
        fields.reshape(channels + 1, rows_ext * col_count),
        field_weight,
        preferred_element_type=jnp.float32,
    ).astype(jnp.bfloat16)
    own = lax.slice_in_dim(embedded, MARGIN * col_count, MARGIN * col_count + cells, axis=0)
    query = jnp.dot(own, qkv_weight[:, 0], preferred_element_type=jnp.float32)
    key = jnp.dot(embedded, qkv_weight[:, 1], preferred_element_type=jnp.float32)
    value = jnp.dot(embedded, qkv_weight[:, 2], preferred_element_type=jnp.float32).astype(
        jnp.bfloat16
    )
    band = jnp.stack([band_start, jnp.int32(total_rows)]).astype(jnp.int32)
    heads_out = window_attend(
        query, key, value, head_shift, logit_scale, band, row_count, col_count, head_dim
    )
    out_proj = jnp.dot(out_weight, proj_weight, preferred_element_type=jnp.float32)
    noise_part = jnp.einsum(
        "mc,rm->cr",
        out_proj,
        heads_out.astype(jnp.float32),
        precision=lax.Precision.HIGHEST,
    ).reshape(channels, row_count, col_count)
    noise = noise_everywhere(noise_part)
    near = slice((MARGIN - HALO) * col_count, (MARGIN + row_count + HALO) * col_count)
    noise = noise + jnp.einsum(
        "dc,rd->cr", proj_weight, embedded[near], preferred_element_type=jnp.float32
    ).reshape(channels, row_count + 2 * HALO, col_count)
    latent_near = fields[:channels, MARGIN - HALO : MARGIN + row_count + HALO]
    stepped = (keep_factor * latent_near.astype(jnp.float32) + noise_factor * noise).astype(
        jnp.bfloat16
    )
    tile_cols = col_count // lax.axis_size("narrow")
    col_start = lax.axis_index("narrow") * tile_cols
    stepped = jnp.pad(stepped, ((0, 0), (0, 0), (HALO, HALO)))
    stepped = lax.dynamic_slice_in_dim(stepped, col_start, tile_cols + 2 * HALO, 2)

    hidden = jax.nn.silu(conv_valid(jnp.transpose(stepped, (1, 2, 0)), conv_in_weight))
    hidden = hidden.astype(jnp.bfloat16)
    scale = 1
    for weight in (None, level_one_weight, level_two_weight, level_three_weight):
        if weight is not None:
            hidden = grow(hidden, corner_weight(weight))
            scale = 2 * scale
        mask = inside_mask(
            hidden.shape[0],
            hidden.shape[1],
            band_start * scale - 1,
            col_start * scale - 1,
            total_rows * scale,
            col_count * scale,
        )
        hidden = jnp.where(mask, hidden, jnp.zeros_like(hidden))
    return conv_final(hidden, conv_out_weight)


def solution(mesh):
    in_specs = (
        P(None, "wide", None),
        P("wide", None),
        P("narrow", None),
        P("narrow"),
        P(),
        P(),
        P(None, None, "narrow"),
        P("narrow", None),
        P(),
        P(),
        P(),
        P(),
        P(),
        P(),
    )
    out_specs = P(None, "wide", "narrow")
    return jax.shard_map(shards, mesh=mesh, in_specs=in_specs, out_specs=out_specs, check_vma=False)
```

```python
import functools
import math

import jax
import jax.numpy as jnp
from jax import lax
from jax.experimental import pallas as pl
from jax.experimental.pallas import tpu as pltpu
from jax.sharding import PartitionSpec as P

WIN = 7
REACH = (WIN - 1) // 2
MARGIN = REACH + 1
HALO = 2


plan_now = 0.3
plan_next = 0.5
keep_factor = math.sqrt(plan_next / plan_now)
noise_factor = math.sqrt(1.0 - plan_next) - keep_factor * math.sqrt(1.0 - plan_now)


def neighbour_rows(cells, width, dim):
    count = lax.axis_size("wide")
    head = lax.slice_in_dim(cells, 0, width, axis=dim)
    tail = lax.slice_in_dim(cells, cells.shape[dim] - width, cells.shape[dim], axis=dim)
    above = lax.ppermute(tail, "wide", [(i, i + 1) for i in range(count - 1)])
    below = lax.ppermute(head, "wide", [(i + 1, i) for i in range(count - 1)])
    return jnp.concatenate([above, cells, below], axis=dim)


def attend_kernel(
    row_count,
    col_count,
    head_dim,
    group,
    shift_ref,
    scale_ref,
    band_ref,
    query_ref,
    key_ref,
    value_ref,
    out_ref,
    query_split,
    key_split,
):
    step = pl.program_id(0)
    span = WIN * col_count
    col_step = lax.broadcasted_iota(jnp.int32, (col_count, col_count), 1) - lax.broadcasted_iota(
        jnp.int32, (col_count, col_count), 0
    )

    def unit(x):
        return x * lax.rsqrt(jnp.sum(x * x, axis=1, keepdims=True) + 1e-06)

    def halves(x):
        high = x.astype(jnp.bfloat16)
        return high, (x - high.astype(jnp.float32)).astype(jnp.bfloat16)

    for slot in range(group):
        head = step * group + slot
        lanes = slice(slot * head_dim, (slot + 1) * head_dim)
        shift_row = shift_ref[head, 0]
        shift_col = shift_ref[head, 1]
        q_high, q_low = halves(unit(query_ref[:, lanes]) * scale_ref[head])
        k_high, k_low = halves(unit(key_ref[:, lanes]))
        query_split[...] = jnp.concatenate([q_high, q_low, q_high, q_low], axis=1)
        key_split[...] = jnp.concatenate([k_high, k_high, k_low, k_low], axis=1)
        offset = col_step - shift_col
        col_bias = jnp.where((offset >= -REACH) & (offset <= REACH), 0.0, -1e30)
        for row in range(row_count):
            start = pl.multiple_of((row + shift_row + (MARGIN - REACH)) * col_count, col_count)
            scores = lax.dot_general(
                query_split[row * col_count : (row + 1) * col_count, :],
                key_split[pl.ds(start, span), :],
                (((1,), (1,)), ((), ())),
                preferred_element_type=jnp.float32,
            )
            first = band_ref[0] + row + shift_row - REACH
            pieces = []
            for k in range(WIN):
                inside = (first + k >= 0) & (first + k < band_ref[1])
                pieces.append(
                    scores[:, k * col_count : (k + 1) * col_count]
                    + (col_bias + jnp.where(inside, 0.0, -1e30))
                )
            peak = jnp.max(functools.reduce(jnp.maximum, pieces), axis=1, keepdims=True)
            pieces = [jnp.exp(piece - peak) for piece in pieces]
            total = jnp.sum(functools.reduce(jnp.add, pieces), axis=1, keepdims=True)
            norm = 1.0 / total
            weights = jnp.concatenate(
                [(piece * norm).astype(jnp.bfloat16) for piece in pieces], axis=1
            )
            mixed = jnp.dot(
                weights, value_ref[pl.ds(start, span), lanes], preferred_element_type=jnp.float32
            )
            out_ref[row * col_count : (row + 1) * col_count, lanes] = mixed.astype(jnp.bfloat16)


def window_attend(query, key, value, shifts, scales, band, row_count, col_count, head_dim):
    heads_here = shifts.shape[0]
    group = 2 if heads_here % 2 == 0 else 1
    width = group * head_dim
    cells = row_count * col_count
    cells_ext = key.shape[0]
    smem = pl.BlockSpec(memory_space=pltpu.SMEM)
    return pl.pallas_call(
        functools.partial(attend_kernel, row_count, col_count, head_dim, group),
        out_shape=jax.ShapeDtypeStruct((cells, heads_here * head_dim), jnp.bfloat16),
        grid=(heads_here // group,),
        in_specs=[
            smem,
            smem,
            smem,
            pl.BlockSpec((cells, width), lambda i: (0, i)),
            pl.BlockSpec((cells_ext, width), lambda i: (0, i)),
            pl.BlockSpec((cells_ext, width), lambda i: (0, i)),
        ],
        out_specs=pl.BlockSpec((cells, width), lambda i: (0, i)),
        scratch_shapes=[
            pltpu.VMEM((cells, 4 * head_dim), jnp.bfloat16),
            pltpu.VMEM((cells_ext, 4 * head_dim), jnp.bfloat16),
        ],
        name="window_attend",
    )(shifts, scales, band, query, key, value)


def grow_kernel(phases, row_total, col_total, base_ref, field_ref, turned_ref, weight_ref, out_ref, taps):
    odd = pl.program_id(0)
    depth, width = weight_ref.shape[2], weight_ref.shape[3]
    rows, stride = out_ref.shape[1], out_ref.shape[3]
    chunk = min(depth, 64)
    first = jnp.where(odd == 0, 1.0, 0.0)

    def combine(index, carry):
        start = pl.multiple_of(index * chunk, chunk)
        for a in range(2):
            edge = []
            for b in range(3):
                middle = weight_ref[1, b, pl.ds(start, chunk), :].astype(jnp.float32)
                outer = weight_ref[2 * a, b, pl.ds(start, chunk), :].astype(jnp.float32)
                edge.append(outer + middle * (first if a == 0 else 1.0 - first))
            left = jnp.concatenate([edge[0] + edge[1], edge[0]], axis=1)
            right = jnp.concatenate([edge[2], edge[1] + edge[2]], axis=1)
            taps[pl.ds(2 * a * depth + start, chunk), :] = left.astype(jnp.bfloat16)
            taps[pl.ds((2 * a + 1) * depth + start, chunk), :] = right.astype(jnp.bfloat16)
        return carry

    lax.fori_loop(0, depth // chunk, combine, 0)
    row_index = (
        2 * lax.broadcasted_iota(jnp.int32, (rows, stride, 1), 0) + odd + base_ref[0]
    )
    col_step = lax.broadcasted_iota(jnp.int32, (rows, stride, 1), 1)
    row_in = (row_index >= 0) & (row_index < row_total)
    for p in range(phases):
        def near(a):
            here = field_ref[p, a : a + rows]
            after = field_ref[p + 1, a : a + rows] if p < phases - 1 else turned_ref[a : a + rows]
            return [piece.reshape(rows * stride, depth) for piece in (here, after)]

        lhs = jnp.concatenate(near(0) + near(1), axis=1)
        total = jnp.dot(lhs, taps[...], preferred_element_type=jnp.float32)
        total = total.reshape(rows, stride, 2 * width)
        for side in range(2):
            value = total[:, :, side * width : (side + 1) * width]
            value = value / (1.0 + jnp.exp(-value))
            col_index = 2 * phases * col_step + (2 * p + side) + base_ref[1]
            inside = row_in & (col_index >= 0) & (col_index < col_total)
            out_ref[2 * p + side, :, 0] = jnp.where(inside, value, 0.0).astype(jnp.bfloat16)


def grow(field_in, weight, base, row_total, col_total):
    phases, rows, stride, depth = field_in.shape
    width = weight.shape[3]
    turned = jnp.roll(field_in[0], -1, axis=1)
    whole = pl.BlockSpec(memory_space=pltpu.VMEM)
    out = pl.pallas_call(
        functools.partial(grow_kernel, phases, row_total, col_total),
        out_shape=jax.ShapeDtypeStruct((2 * phases, rows - 1, 2, stride, width), jnp.bfloat16),
        grid=(2,),
        in_specs=[pl.BlockSpec(memory_space=pltpu.SMEM), whole, whole, whole],
        out_specs=pl.BlockSpec((2 * phases, rows - 1, 1, stride, width), lambda i: (0, 0, i, 0, 0)),
        scratch_shapes=[pltpu.VMEM((4 * depth, 2 * width), jnp.bfloat16)],
        name="grow",
    )(base, field_in, turned, weight)
    return out.reshape(2 * phases, 2 * (rows - 1), stride, width)


def conv_valid(padded, weight):
    return lax.conv_general_dilated(
        padded[None],
        weight,
        (1, 1),
        "VALID",
        dimension_numbers=("NHWC", "HWIO", "NHWC"),
        preferred_element_type=jnp.float32,
    )[0]


def inside_mask(rows, cols, row_first, col_first, row_total, col_total):
    row_index = row_first + jnp.arange(rows, dtype=jnp.int32)
    col_index = col_first + jnp.arange(cols, dtype=jnp.int32)
    row_in = (row_index >= 0) & (row_index < row_total)
    col_in = (col_index >= 0) & (col_index < col_total)
    return (row_in[:, None] & col_in[None, :])[:, :, None]


def conv_final(field_in, weight, rows, cols):
    phases, rows_in, stride, depth = field_in.shape
    out_vars = weight.shape[3]
    steps = cols // phases
    taps = jnp.transpose(weight, (0, 1, 3, 2)).reshape(9 * out_vars, depth)
    parts = lax.dot_general(
        taps,
        field_in.reshape(phases * rows_in * stride, depth),
        (((1,), (1,)), ((), ())),
        preferred_element_type=jnp.float32,
    ).reshape(3, 3, out_vars, phases, rows_in, stride)
    strips = []
    for q in range(phases):
        strip = jnp.zeros((out_vars, rows, steps), jnp.float32)
        for a in range(3):
            for b in range(3):
                p, skip = (q + b) % phases, (q + b) // phases
                strip = strip + parts[a, b, :, p, a : a + rows, skip : skip + steps]
        strips.append(strip)
    strips = jnp.concatenate(strips, axis=2)
    source = lax.broadcasted_iota(jnp.int32, (cols, cols), 0)
    target = lax.broadcasted_iota(jnp.int32, (cols, cols), 1)
    order = (source % steps) * phases + source // steps == target
    return jnp.einsum(
        "vrs,st->vrt", strips, order.astype(jnp.float32), precision=lax.Precision.HIGHEST
    )


def noise_everywhere(part):
    wide = lax.axis_size("wide")
    narrow = lax.axis_size("narrow")
    rows = part.shape[1]
    pieces = {
        1: lax.slice_in_dim(part, rows - HALO, rows, axis=1),
        0: part,
        -1: lax.slice_in_dim(part, 0, HALO, axis=1),
    }
    sums = {}
    for move in (0, 1, -1):
        total = part if move == 0 else None
        for turn in range(narrow):
            if move == 0 and turn == 0:
                continue
            pairs = [
                (w * narrow + n, (w + move) * narrow + (n + turn) % narrow)
                for w in range(wide)
                for n in range(narrow)
                if 0 <= w + move < wide
            ]
            arrived = lax.ppermute(pieces[move], ("wide", "narrow"), pairs)
            total = arrived if total is None else total + arrived
        sums[move] = total
    return jnp.concatenate([sums[1], sums[0], sums[-1]], axis=1)


def shards(
    latent,
    land_sea,
    head_shift,
    logit_scale,
    embed_weight,
    land_vector,
    qkv_weight,
    out_weight,
    proj_weight,
    conv_in_weight,
    level_one_weight,
    level_two_weight,
    level_three_weight,
    conv_out_weight,
):
    channels, row_count, col_count = latent.shape
    heads_here = head_shift.shape[0]
    head_dim = qkv_weight.shape[2] // heads_here
    cells = row_count * col_count
    band_start = lax.axis_index("wide") * row_count
    total_rows = row_count * lax.axis_size("wide")

    fields = jnp.concatenate([latent, land_sea.astype(jnp.bfloat16)[None]], axis=0)
    fields = neighbour_rows(fields, MARGIN, 1)
    field_weight = jnp.concatenate([embed_weight, land_vector[None]], axis=0)
    rows_ext = row_count + 2 * MARGIN
    embedded = jnp.einsum(
        "cm,cd->md",
        fields.reshape(channels + 1, rows_ext * col_count),
        field_weight,
        preferred_element_type=jnp.float32,
    ).astype(jnp.bfloat16)
    own = lax.slice_in_dim(embedded, MARGIN * col_count, MARGIN * col_count + cells, axis=0)
    query = jnp.dot(own, qkv_weight[:, 0], preferred_element_type=jnp.float32)
    key = jnp.dot(embedded, qkv_weight[:, 1], preferred_element_type=jnp.float32)
    value = jnp.dot(embedded, qkv_weight[:, 2], preferred_element_type=jnp.float32).astype(
        jnp.bfloat16
    )
    band = jnp.stack([band_start, jnp.int32(total_rows)]).astype(jnp.int32)
    heads_out = window_attend(
        query, key, value, head_shift, logit_scale, band, row_count, col_count, head_dim
    )
    out_proj = jnp.dot(out_weight, proj_weight, preferred_element_type=jnp.float32)
    noise_part = jnp.einsum(
        "mc,rm->cr",
        out_proj,
        heads_out.astype(jnp.float32),
        precision=lax.Precision.HIGHEST,
    ).reshape(channels, row_count, col_count)
    noise = noise_everywhere(noise_part)
    near = slice((MARGIN - HALO) * col_count, (MARGIN + row_count + HALO) * col_count)
    noise = noise + jnp.einsum(
        "dc,rd->cr", proj_weight, embedded[near], preferred_element_type=jnp.float32
    ).reshape(channels, row_count + 2 * HALO, col_count)
    latent_near = fields[:channels, MARGIN - HALO : MARGIN + row_count + HALO]
    stepped = (keep_factor * latent_near.astype(jnp.float32) + noise_factor * noise).astype(
        jnp.bfloat16
    )
    tile_cols = col_count // lax.axis_size("narrow")
    col_start = lax.axis_index("narrow") * tile_cols
    stepped = jnp.pad(stepped, ((0, 0), (0, 0), (HALO, HALO)))
    stepped = lax.dynamic_slice_in_dim(stepped, col_start, tile_cols + 2 * HALO, 2)

    hidden = jax.nn.silu(conv_valid(jnp.transpose(stepped, (1, 2, 0)), conv_in_weight))
    hidden = hidden.astype(jnp.bfloat16)
    mask = inside_mask(
        hidden.shape[0], hidden.shape[1], band_start - 1, col_start - 1, total_rows, col_count
    )
    hidden = jnp.where(mask, hidden, jnp.zeros_like(hidden))
    spare = -hidden.shape[1] % 16
    hidden = jnp.pad(hidden, ((0, 0), (0, spare), (0, 0)))[None]
    scale = 1
    for weight in (level_one_weight, level_two_weight, level_three_weight):
        scale = 2 * scale
        base = jnp.stack([band_start * scale - 1, col_start * scale - 1]).astype(jnp.int32)
        hidden = grow(hidden, weight, base, total_rows * scale, col_count * scale)
    return conv_final(hidden, conv_out_weight, row_count * scale, tile_cols * scale)


def solution(mesh):
    in_specs = (
        P(None, "wide", None),
        P("wide", None),
        P("narrow", None),
        P("narrow"),
        P(),
        P(),
        P(None, None, "narrow"),
        P("narrow", None),
        P(),
        P(),
        P(),
        P(),
        P(),
        P(),
    )
    out_specs = P(None, "wide", "narrow")
    return jax.shard_map(shards, mesh=mesh, in_specs=in_specs, out_specs=out_specs, check_vma=False)
```

```python
import functools
import math

import jax
import jax.numpy as jnp
from jax import lax
from jax.experimental import pallas as pl
from jax.experimental.pallas import tpu as pltpu
from jax.sharding import PartitionSpec as P

WIN = 7
REACH = (WIN - 1) // 2
MARGIN = REACH + 1
HALO = 2


plan_now = 0.3
plan_next = 0.5
keep_factor = math.sqrt(plan_next / plan_now)
noise_factor = math.sqrt(1.0 - plan_next) - keep_factor * math.sqrt(1.0 - plan_now)


def neighbour_rows(cells, width, dim):
    count = lax.axis_size("wide")
    head = lax.slice_in_dim(cells, 0, width, axis=dim)
    tail = lax.slice_in_dim(cells, cells.shape[dim] - width, cells.shape[dim], axis=dim)
    above = lax.ppermute(tail, "wide", [(i, i + 1) for i in range(count - 1)])
    below = lax.ppermute(head, "wide", [(i + 1, i) for i in range(count - 1)])
    return jnp.concatenate([above, cells, below], axis=dim)


def attend_kernel(
    row_count,
    col_count,
    head_dim,
    group,
    shift_ref,
    scale_ref,
    band_ref,
    query_ref,
    key_ref,
    value_ref,
    out_ref,
    query_split,
    key_split,
):
    step = pl.program_id(0)
    span = WIN * col_count
    col_step = lax.broadcasted_iota(jnp.int32, (col_count, col_count), 1) - lax.broadcasted_iota(
        jnp.int32, (col_count, col_count), 0
    )

    def unit(x):
        return x * lax.rsqrt(jnp.sum(x * x, axis=1, keepdims=True) + 1e-06)

    def halves(x):
        high = x.astype(jnp.bfloat16)
        return high, (x - high.astype(jnp.float32)).astype(jnp.bfloat16)

    for slot in range(group):
        head = step * group + slot
        lanes = slice(slot * head_dim, (slot + 1) * head_dim)
        shift_row = shift_ref[head, 0]
        shift_col = shift_ref[head, 1]
        q_high, q_low = halves(unit(query_ref[:, lanes]) * scale_ref[head])
        k_high, k_low = halves(unit(key_ref[:, lanes]))
        query_split[...] = jnp.concatenate([q_high, q_low, q_high, q_low], axis=1)
        key_split[...] = jnp.concatenate([k_high, k_high, k_low, k_low], axis=1)
        offset = col_step - shift_col
        col_bias = jnp.where((offset >= -REACH) & (offset <= REACH), 0.0, -1e30)
        for row in range(row_count):
            start = pl.multiple_of((row + shift_row + (MARGIN - REACH)) * col_count, col_count)
            scores = lax.dot_general(
                query_split[row * col_count : (row + 1) * col_count, :],
                key_split[pl.ds(start, span), :],
                (((1,), (1,)), ((), ())),
                preferred_element_type=jnp.float32,
            )
            first = band_ref[0] + row + shift_row - REACH
            pieces = []
            for k in range(WIN):
                inside = (first + k >= 0) & (first + k < band_ref[1])
                pieces.append(
                    scores[:, k * col_count : (k + 1) * col_count]
                    + (col_bias + jnp.where(inside, 0.0, -1e30))
                )
            peak = jnp.max(functools.reduce(jnp.maximum, pieces), axis=1, keepdims=True)
            pieces = [jnp.exp(piece - peak) for piece in pieces]
            total = jnp.sum(functools.reduce(jnp.add, pieces), axis=1, keepdims=True)
            norm = 1.0 / total
            weights = jnp.concatenate(
                [(piece * norm).astype(jnp.bfloat16) for piece in pieces], axis=1
            )
            mixed = jnp.dot(
                weights, value_ref[pl.ds(start, span), lanes], preferred_element_type=jnp.float32
            )
            out_ref[row * col_count : (row + 1) * col_count, lanes] = mixed.astype(jnp.bfloat16)


def window_attend(query, key, value, shifts, scales, band, row_count, col_count, head_dim):
    heads_here = shifts.shape[0]
    group = 2 if heads_here % 2 == 0 else 1
    width = group * head_dim
    cells = row_count * col_count
    cells_ext = key.shape[0]
    smem = pl.BlockSpec(memory_space=pltpu.SMEM)
    return pl.pallas_call(
        functools.partial(attend_kernel, row_count, col_count, head_dim, group),
        out_shape=jax.ShapeDtypeStruct((cells, heads_here * head_dim), jnp.bfloat16),
        grid=(heads_here // group,),
        in_specs=[
            smem,
            smem,
            smem,
            pl.BlockSpec((cells, width), lambda i: (0, i)),
            pl.BlockSpec((cells_ext, width), lambda i: (0, i)),
            pl.BlockSpec((cells_ext, width), lambda i: (0, i)),
        ],
        out_specs=pl.BlockSpec((cells, width), lambda i: (0, i)),
        scratch_shapes=[
            pltpu.VMEM((cells, 4 * head_dim), jnp.bfloat16),
            pltpu.VMEM((cells_ext, 4 * head_dim), jnp.bfloat16),
        ],
        name="window_attend",
    )(shifts, scales, band, query, key, value)


def grow_kernel(phases, row_total, col_total, base_ref, field_ref, weight_ref, out_ref, taps):
    odd = pl.program_id(0)
    depth, width = weight_ref.shape[2], weight_ref.shape[3]
    rows, stride = out_ref.shape[1], out_ref.shape[3]
    chunk = min(depth, 64)
    first = jnp.where(odd == 0, 1.0, 0.0)

    def combine(index, carry):
        start = pl.multiple_of(index * chunk, chunk)
        for a in range(2):
            edge = []
            for b in range(3):
                middle = weight_ref[1, b, pl.ds(start, chunk), :].astype(jnp.float32)
                outer = weight_ref[2 * a, b, pl.ds(start, chunk), :].astype(jnp.float32)
                edge.append(outer + middle * (first if a == 0 else 1.0 - first))
            left = jnp.concatenate([edge[0] + edge[1], edge[0]], axis=1)
            right = jnp.concatenate([edge[2], edge[1] + edge[2]], axis=1)
            taps[pl.ds(2 * a * depth + start, chunk), :] = left.astype(jnp.bfloat16)
            taps[pl.ds((2 * a + 1) * depth + start, chunk), :] = right.astype(jnp.bfloat16)
        return carry

    lax.fori_loop(0, depth // chunk, combine, 0)
    row_index = (
        2 * lax.broadcasted_iota(jnp.int32, (rows, stride, 1), 0) + odd + base_ref[0]
    )
    col_step = lax.broadcasted_iota(jnp.int32, (rows, stride, 1), 1)
    row_in = (row_index >= 0) & (row_index < row_total)
    for p in range(phases):
        def near(a):
            here = field_ref[p, a : a + rows].reshape(rows * stride, depth)
            if p < phases - 1:
                after = field_ref[p + 1, a : a + rows].reshape(rows * stride, depth)
            else:
                after = field_ref[0, a : a + rows].reshape(rows * stride, depth)
                after = pltpu.roll(after.astype(jnp.float32), rows * stride - 1, 0)
                after = after.astype(jnp.bfloat16)
            return [here, after]

        lhs = jnp.concatenate(near(0) + near(1), axis=1)
        total = jnp.dot(lhs, taps[...], preferred_element_type=jnp.float32)
        total = total.reshape(rows, stride, 2 * width)
        for side in range(2):
            value = total[:, :, side * width : (side + 1) * width]
            value = value / (1.0 + jnp.exp(-value))
            col_index = 2 * phases * col_step + (2 * p + side) + base_ref[1]
            inside = row_in & (col_index >= 0) & (col_index < col_total)
            out_ref[2 * p + side, :, 0] = jnp.where(inside, value, 0.0).astype(jnp.bfloat16)


def grow(field_in, weight, base, row_total, col_total):
    phases, rows, stride, depth = field_in.shape
    width = weight.shape[3]
    whole = pl.BlockSpec(memory_space=pltpu.VMEM)
    out = pl.pallas_call(
        functools.partial(grow_kernel, phases, row_total, col_total),
        out_shape=jax.ShapeDtypeStruct((2 * phases, rows - 1, 2, stride, width), jnp.bfloat16),
        grid=(2,),
        in_specs=[pl.BlockSpec(memory_space=pltpu.SMEM), whole, whole],
        out_specs=pl.BlockSpec((2 * phases, rows - 1, 1, stride, width), lambda i: (0, 0, i, 0, 0)),
        scratch_shapes=[pltpu.VMEM((4 * depth, 2 * width), jnp.bfloat16)],
        name="grow",
    )(base, field_in, weight)
    return out.reshape(2 * phases, 2 * (rows - 1), stride, width)


def conv_valid(padded, weight):
    return lax.conv_general_dilated(
        padded[None],
        weight,
        (1, 1),
        "VALID",
        dimension_numbers=("NHWC", "HWIO", "NHWC"),
        preferred_element_type=jnp.float32,
    )[0]


def inside_mask(rows, cols, row_first, col_first, row_total, col_total):
    row_index = row_first + jnp.arange(rows, dtype=jnp.int32)
    col_index = col_first + jnp.arange(cols, dtype=jnp.int32)
    row_in = (row_index >= 0) & (row_index < row_total)
    col_in = (col_index >= 0) & (col_index < col_total)
    return (row_in[:, None] & col_in[None, :])[:, :, None]


def conv_final(field_in, weight, rows, cols):
    phases, rows_in, stride, depth = field_in.shape
    out_vars = weight.shape[3]
    steps = cols // phases
    taps = jnp.transpose(weight, (0, 1, 3, 2)).reshape(9 * out_vars, depth)
    parts = jnp.einsum("kd,prsd->kprs", taps, field_in, preferred_element_type=jnp.float32)
    parts = parts.reshape(3, 3, out_vars, phases, rows_in, stride)
    strips = []
    for q in range(phases):
        strip = jnp.zeros((out_vars, rows, steps), jnp.float32)
        for a in range(3):
            for b in range(3):
                p, skip = (q + b) % phases, (q + b) // phases
                strip = strip + parts[a, b, :, p, a : a + rows, skip : skip + steps]
        strips.append(strip)
    strips = jnp.concatenate(strips, axis=2)
    source = lax.broadcasted_iota(jnp.int32, (cols, cols), 0)
    target = lax.broadcasted_iota(jnp.int32, (cols, cols), 1)
    order = (source % steps) * phases + source // steps == target
    return jnp.einsum(
        "vrs,st->vrt", strips, order.astype(jnp.float32), precision=lax.Precision.HIGHEST
    )


def noise_everywhere(part):
    narrow = lax.axis_size("narrow")
    total = part
    for turn in range(1, narrow):
        total = total + lax.ppermute(
            part, "narrow", [(n, (n + turn) % narrow) for n in range(narrow)]
        )
    return neighbour_rows(total, HALO, 1)


def shards(
    latent,
    land_sea,
    head_shift,
    logit_scale,
    embed_weight,
    land_vector,
    qkv_weight,
    out_weight,
    proj_weight,
    conv_in_weight,
    level_one_weight,
    level_two_weight,
    level_three_weight,
    conv_out_weight,
):
    channels, row_count, col_count = latent.shape
    heads_here = head_shift.shape[0]
    head_dim = qkv_weight.shape[2] // heads_here
    cells = row_count * col_count
    band_start = lax.axis_index("wide") * row_count
    total_rows = row_count * lax.axis_size("wide")

    fields = jnp.concatenate([latent, land_sea.astype(jnp.bfloat16)[None]], axis=0)
    fields = neighbour_rows(fields, MARGIN, 1)
    field_weight = jnp.concatenate([embed_weight, land_vector[None]], axis=0)
    rows_ext = row_count + 2 * MARGIN
    embedded = jnp.einsum(
        "cm,cd->md",
        fields.reshape(channels + 1, rows_ext * col_count),
        field_weight,
        preferred_element_type=jnp.float32,
    ).astype(jnp.bfloat16)
    own = lax.slice_in_dim(embedded, MARGIN * col_count, MARGIN * col_count + cells, axis=0)
    query = jnp.dot(own, qkv_weight[:, 0], preferred_element_type=jnp.float32)
    key = jnp.dot(embedded, qkv_weight[:, 1], preferred_element_type=jnp.float32)
    value = jnp.dot(embedded, qkv_weight[:, 2], preferred_element_type=jnp.float32).astype(
        jnp.bfloat16
    )
    band = jnp.stack([band_start, jnp.int32(total_rows)]).astype(jnp.int32)
    heads_out = window_attend(
        query, key, value, head_shift, logit_scale, band, row_count, col_count, head_dim
    )
    out_proj = jnp.dot(out_weight, proj_weight, preferred_element_type=jnp.float32)
    noise_part = jnp.einsum(
        "mc,rm->cr",
        out_proj,
        heads_out.astype(jnp.float32),
        precision=lax.Precision.HIGHEST,
    ).reshape(channels, row_count, col_count)
    noise = noise_everywhere(noise_part)
    near = slice((MARGIN - HALO) * col_count, (MARGIN + row_count + HALO) * col_count)
    noise = noise + jnp.einsum(
        "dc,rd->cr", proj_weight, embedded[near], preferred_element_type=jnp.float32
    ).reshape(channels, row_count + 2 * HALO, col_count)
    latent_near = fields[:channels, MARGIN - HALO : MARGIN + row_count + HALO]
    stepped = (keep_factor * latent_near.astype(jnp.float32) + noise_factor * noise).astype(
        jnp.bfloat16
    )
    tile_cols = col_count // lax.axis_size("narrow")
    col_start = lax.axis_index("narrow") * tile_cols
    stepped = jnp.pad(stepped, ((0, 0), (0, 0), (HALO, HALO)))
    stepped = lax.dynamic_slice_in_dim(stepped, col_start, tile_cols + 2 * HALO, 2)

    hidden = jax.nn.silu(conv_valid(jnp.transpose(stepped, (1, 2, 0)), conv_in_weight))
    hidden = hidden.astype(jnp.bfloat16)
    mask = inside_mask(
        hidden.shape[0], hidden.shape[1], band_start - 1, col_start - 1, total_rows, col_count
    )
    hidden = jnp.where(mask, hidden, jnp.zeros_like(hidden))
    spare = -hidden.shape[1] % 16
    hidden = jnp.pad(hidden, ((0, 0), (0, spare), (0, 0)))[None]
    scale = 1
    for weight in (level_one_weight, level_two_weight, level_three_weight):
        scale = 2 * scale
        base = jnp.stack([band_start * scale - 1, col_start * scale - 1]).astype(jnp.int32)
        hidden = grow(hidden, weight, base, total_rows * scale, col_count * scale)
    return conv_final(hidden, conv_out_weight, row_count * scale, tile_cols * scale)


def solution(mesh):
    in_specs = (
        P(None, "wide", None),
        P("wide", None),
        P("narrow", None),
        P("narrow"),
        P(),
        P(),
        P(None, None, "narrow"),
        P("narrow", None),
        P(),
        P(),
        P(),
        P(),
        P(),
        P(),
    )
    out_specs = P(None, "wide", "narrow")
    return jax.shard_map(shards, mesh=mesh, in_specs=in_specs, out_specs=out_specs, check_vma=False)
```
